128 devices in a mesh: grp: 8 (over y, core), wide: 16 (over z, x).
Axes of the slice: x: 4, y: 4, z: 4, core: 2. Of those that a mesh axis runs over, the one named last changes fastest.
Arguments:
- coefficients: bfloat16 [2048, 2, 128, 512], P(('grp', 'wide')), may hold values from -6 to 6
- source_blocks: bfloat16 [2, 2048, 2, 128, 256], P(None, ('grp', 'wide')), may hold values from -0.25 to 0.25
- target_blocks: bfloat16 [3, 2048, 2, 128, 256], P(None, ('grp', 'wide')), may hold values from -0.25 to 0.25
- pair_tables: int32 [2, 128, 16], P(None, ('grp', 'wide')), may hold values from 0 to 15, each once within a row
Outputs:
- target_coeffs: bfloat16 [2048, 2, 128, 512], P(('grp', 'wide'))
The draws below stay inside these ranges and needn't reach their ends.
Inputs may be any that keep to these rules, and one draw needn't show every extreme that they name: Each row pair_tables[s, d] is a permutation of the numbers 0 to 15.
All inputs are finite; a program needn't handle non-finite values.
Results may differ from the reference program's by a relative error of at most 0.007.
Values may be sent and summed in bfloat16 or wider, within the bound.
No kernel may reach another device: no remote copies, remote signals or barrier semaphores. Data moves between devices by JAX's collectives and lax.ppermute only.
A program may use at most 128 MiB of HBM per device.

```python
import jax
import jax.numpy as jnp
import numpy as np
from jax import lax

R = 128
E = 512
BOX_DEV = 16
SRC_LEVELS = 2
TGT_LEVELS = 3
P_SIZE = 2048
N_GRP = 8
N_WIDE = 16
DEVICES = 128


def shard_levels(own_key, dims, cuts, low, largest):
    factor_of = 1.0
    for dim, blocks in cuts:
        draws = jax.random.uniform(jax.random.fold_in(jax.random.fold_in(own_key, 6), dim), (blocks,), jnp.float32, low / len(cuts), largest / len(cuts))
        factor_of = factor_of * jnp.repeat(jnp.exp(draws), dims[dim] // blocks).reshape((-1,) + (1,) * (len(dims) - 1 - dim))
    return factor_of


def scatter_about(key, dims, deviation, reach, shards=(), kind=jnp.bfloat16):
    values = jax.random.normal(key, dims, jnp.float32) * deviation
    if len(shards) > 0:
        values = shard_levels(key, dims, shards, -0.22, 0.18) * values
    return jnp.clip(values, min=-reach, max=reach).astype(kind)


def setup_inputs(seed: int = 0) -> dict:
    seeds = jax.random.split(jax.random.key(seed), 5)
    coefficients = scatter_about(seeds[0], (P_SIZE, 2, R, E), 1.0, 6.0, ((0, 128),))
    source_blocks = scatter_about(seeds[1], (SRC_LEVELS, P_SIZE, 2, R, 2 * R), (4 * R) ** -0.5, 0.25, ((1, 128),))
    target_blocks = scatter_about(seeds[2], (TGT_LEVELS, P_SIZE, 2, R, 2 * R), (4 * R) ** -0.5, 0.25, ((1, 128),))
    pair_tables = jax.vmap(lambda own: jax.random.permutation(own, BOX_DEV))(jax.random.split(seeds[3], SRC_LEVELS * DEVICES)).reshape((SRC_LEVELS, DEVICES, BOX_DEV)).astype(jnp.int32)
    return dict(coefficients=coefficients, source_blocks=source_blocks, target_blocks=target_blocks, pair_tables=pair_tables)


def complex_apply(blocks, stacked):
    matrix = blocks.astype(jnp.float32)
    vector = stacked.astype(jnp.float32)
    real_part = jnp.einsum('nij,njk->nik', matrix[:, 0], vector[:, 0]) - jnp.einsum('nij,njk->nik', matrix[:, 1], vector[:, 1])
    imag_part = jnp.einsum('nij,njk->nik', matrix[:, 0], vector[:, 1]) + jnp.einsum('nij,njk->nik', matrix[:, 1], vector[:, 0])
    return jnp.stack([real_part, imag_part], axis=1).astype(jnp.bfloat16)


def source_block(operands):
    local_boxes, local_blocks, order_row = operands
    picked = jnp.take(local_boxes, order_row.astype(jnp.int32), axis=0)
    count = picked.shape[0]
    paired = picked.reshape((count // 2, 2) + picked.shape[1:])
    joined = jnp.concatenate([paired[:, 0], paired[:, 1]], axis=2)
    joined = jnp.repeat(joined, 2, axis=0)
    return complex_apply(local_blocks, joined)


def reference(coefficients, source_blocks, target_blocks, pair_tables):
    shape_box = coefficients.shape[1:]
    shape_blk = source_blocks.shape[2:]
    current = coefficients.reshape((DEVICES, BOX_DEV) + shape_box)
    for layer_idx in range(SRC_LEVELS):
        blocks_dev = source_blocks[layer_idx].reshape((DEVICES, BOX_DEV) + shape_blk)
        current = lax.map(source_block, (current, blocks_dev, pair_tables[layer_idx]))
    current = current.reshape((N_GRP, N_WIDE, N_WIDE, BOX_DEV // N_WIDE) + shape_box)
    current = current.transpose(0, 2, 1, 3, 4, 5, 6)
    current = current.reshape((N_GRP, N_WIDE * BOX_DEV) + shape_box)
    bit_count = N_GRP.bit_length() - 1
    groups_all = np.arange(N_GRP)
    for layer_idx in range(TGT_LEVELS):
        mask_bit = 1 << (layer_idx % bit_count)
        lower_ids = jnp.asarray(groups_all & ~mask_bit, dtype=jnp.int32)
        upper_ids = jnp.asarray(groups_all | mask_bit, dtype=jnp.int32)
        blocks_grp = target_blocks[layer_idx].reshape((N_GRP, N_WIDE * BOX_DEV) + shape_blk)
        previous = current

        def target_group(operands):
            lower_id, upper_id, group_blocks = operands
            lower_part = lax.dynamic_index_in_dim(previous, lower_id, 0, keepdims=False)
            upper_part = lax.dynamic_index_in_dim(previous, upper_id, 0, keepdims=False)
            joined = jnp.concatenate([lower_part, upper_part], axis=2)
            return complex_apply(group_blocks, joined)

        current = lax.map(target_group, (lower_ids, upper_ids, blocks_grp))
    return current.reshape((N_GRP * N_WIDE * BOX_DEV,) + shape_box)
```

```python
import functools

import jax
import jax.numpy as jnp
from jax import lax
from jax.experimental import pallas as pl
from jax.experimental.pallas import tpu as pltpu
from jax.sharding import PartitionSpec as P


CHUNKS = (128, 128, 128, 128)
SHIFTS = (1, 3, 2)
VMEM_LIMIT = 8 * 1024 * 1024


def pack_pair(first, second):
    real = jnp.concatenate([first[0], second[0]], axis=0)
    imag = jnp.concatenate([first[1], second[1]], axis=0)
    return jnp.concatenate([real, imag], axis=1)


def block_product(blocks, packed):
    count, _, rank, wide = blocks.shape
    cols = packed.shape[1] // 2
    terms = jnp.dot(
        blocks.reshape(count * 2 * rank, wide), packed, preferred_element_type=jnp.float32
    )
    results = []
    for idx in range(count):
        top = terms[2 * idx * rank : (2 * idx + 1) * rank]
        low = terms[(2 * idx + 1) * rank : (2 * idx + 2) * rank]
        real = top[:, :cols] - low[:, cols:]
        imag = top[:, cols:] + low[:, :cols]
        results.append((real.astype(jnp.bfloat16), imag.astype(jnp.bfloat16)))
    return results


def source_kernel(first_col, order_ref, boxes_ref, blocks_ref, out_ref, middle):
    cols = out_ref.shape[-1]
    count = out_ref.shape[0]
    columns = pl.ds(first_col, cols)
    for level in range(2):
        write = out_ref if level else middle

        def step(pair, _, level=level, write=write):
            base = 2 * pair
            ids = order_ref[level, base], order_ref[level, base + 1]
            if level:
                boxes = [middle[idx] for idx in ids]
            else:
                boxes = [boxes_ref[idx, :, :, columns] for idx in ids]
            packed = pack_pair(*boxes)
            pairs = block_product(blocks_ref[level, pl.ds(base, 2)], packed)
            for idx, (real, imag) in enumerate(pairs):
                write[base + idx, 0] = real
                write[base + idx, 1] = imag
            return 0

        lax.fori_loop(0, count // 2, step, 0, unroll=2)


IN_VMEM = pl.BlockSpec(memory_space=pltpu.VMEM)
IN_SMEM = pl.BlockSpec(memory_space=pltpu.SMEM)


def source_levels(boxes, blocks, order, first_col, cols):
    count, _, rank, _ = boxes.shape
    shape = (count, 2, rank, cols)
    return pl.pallas_call(
        functools.partial(source_kernel, first_col),
        out_shape=jax.ShapeDtypeStruct(shape, jnp.bfloat16),
        in_specs=[IN_SMEM, IN_VMEM, IN_VMEM],
        out_specs=IN_VMEM,
        scratch_shapes=[pltpu.VMEM(shape, jnp.bfloat16)],
        compiler_params=pltpu.CompilerParams(vmem_limit_bytes=VMEM_LIMIT),
        name="source_levels",
    )(order, boxes, blocks)


def core_kernel(place_ref, own_ref, other_ref, blocks_ref, *out_refs):
    row = place_ref[0]
    is_upper = place_ref[1] == 1
    part = out_refs[0].shape[0]
    for shift, out_ref in enumerate(out_refs):
        base = ((row + shift) & 3) * part
        for idx in range(part):
            own, other = own_ref[base + idx], other_ref[base + idx]
            lower = jnp.where(is_upper, other, own)
            upper = jnp.where(is_upper, own, other)
            ((real, imag),) = block_product(
                blocks_ref[pl.ds(base + idx, 1)], pack_pair(lower, upper)
            )
            out_ref[idx, 0] = real
            out_ref[idx, 1] = imag


def core_level(place, own, other, blocks):
    count, _, rank, cols = own.shape
    return pl.pallas_call(
        core_kernel,
        out_shape=[jax.ShapeDtypeStruct((count // 4, 2, rank, cols), jnp.bfloat16)] * 4,
        in_specs=[IN_SMEM, IN_VMEM, IN_VMEM, IN_VMEM],
        out_specs=[IN_VMEM] * 4,
        compiler_params=pltpu.CompilerParams(vmem_limit_bytes=VMEM_LIMIT),
        name="core_level",
    )(place, own, other, blocks)


def slice_kernel(place_ref, blocks_ref, *refs):
    out_refs, sem = refs[:-1], refs[-1]
    row = place_ref[0]
    part = out_refs[0].shape[1]
    copies = []
    for shift, out_ref in enumerate(out_refs):
        start = ((row + shift) & 3) * part
        for level in range(2):
            view = blocks_ref.at[1 + level, pl.ds(start, part)]
            copies.append(
                pltpu.make_async_copy(view, out_ref.at[level], sem.at[shift, level])
            )
            copies[-1].start()
    for copy in copies:
        copy.wait()


def slice_blocks(place, blocks):
    _, count, _, rank, wide = blocks.shape
    shape = (2, count // 4, 2, rank, wide)
    return pl.pallas_call(
        slice_kernel,
        out_shape=[jax.ShapeDtypeStruct(shape, jnp.bfloat16)] * 4,
        in_specs=[IN_SMEM, pl.BlockSpec(memory_space=pltpu.HBM)],
        out_specs=[IN_VMEM] * 4,
        scratch_shapes=[pltpu.SemaphoreType.DMA((4, 2))],
        compiler_params=pltpu.CompilerParams(vmem_limit_bytes=VMEM_LIMIT),
        name="slice_blocks",
    )(place, blocks)


def plane_kernel(place_ref, x0, x1, x2, x3, w0, w1, w2, w3, o0, o1, o2, o3, middle):
    row = place_ref[0]
    part = x0.shape[0]
    states, blocks, outs = (x0, x1, x2, x3), (w0, w1, w2, w3), (o0, o3, o2, o1)

    def pair_blocks(level, first, second, idx):
        return jnp.concatenate(
            [blocks[first][level, pl.ds(idx, 1)], blocks[second][level, pl.ds(idx, 1)]], axis=0
        )

    def first_level(pairs):
        def step(idx, _):
            for low, high in pairs:
                packed = pack_pair(states[low][idx], states[high][idx])
                results = block_product(pair_blocks(0, low, high, idx), packed)
                for source, (real, imag) in zip((low, high), results):
                    plane = (row + 4 - source) & 3
                    middle[plane, idx, 0] = real
                    middle[plane, idx, 1] = imag
            return 0

        lax.fori_loop(0, part, step, 0)

    @pl.when((row & 1) == 0)
    def _():
        first_level(((0, 3), (2, 1)))

    @pl.when((row & 1) == 1)
    def _():
        first_level(((1, 0), (3, 2)))

    def step(idx, _):
        for source in range(2):
            plane = (row + 4 - source) & 1
            packed = pack_pair(middle[plane, idx], middle[plane + 2, idx])
            results = block_product(pair_blocks(1, source, source + 2, idx), packed)
            for target, (real, imag) in zip((source, source + 2), results):
                outs[target][idx, 0] = real
                outs[target][idx, 1] = imag
        return 0

    lax.fori_loop(0, part, step, 0)


def plane_levels(place, states, blocks):
    part, _, rank, cols = states[0].shape
    return pl.pallas_call(
        plane_kernel,
        out_shape=[jax.ShapeDtypeStruct((part, 2, rank, cols), jnp.bfloat16)] * 4,
        in_specs=[IN_SMEM] + [IN_VMEM] * 8,
        out_specs=[IN_VMEM] * 4,
        scratch_shapes=[pltpu.VMEM((4, part, 2, rank, cols), jnp.bfloat16)],
        compiler_params=pltpu.CompilerParams(vmem_limit_bytes=VMEM_LIMIT),
        name="plane_levels",
    )(place, *states, *blocks)


def place_kernel(chunk_cols, place_ref, *refs):
    pieces, out_ref, sem = refs[:-2], refs[-2], refs[-1]
    row = place_ref[0]
    part = pieces[0].shape[0]
    copies = []
    for idx, piece in enumerate(pieces):
        chunk, shift = divmod(idx, 4)
        slot = (row + 4 - shift) & 3
        columns = pl.ds(sum(chunk_cols[:chunk]), chunk_cols[chunk])
        view = out_ref.at[pl.ds(slot * part, part), :, :, columns]
        copies.append(pltpu.make_async_copy(piece, view, sem.at[idx]))
        copies[-1].start()
    for copy in copies:
        copy.wait()


def put_together(place, pieces, chunk_cols):
    part, _, rank, _ = pieces[0].shape
    return pl.pallas_call(
        functools.partial(place_kernel, chunk_cols),
        out_shape=jax.ShapeDtypeStruct((4 * part, 2, rank, sum(chunk_cols)), jnp.bfloat16),
        in_specs=[IN_SMEM] + [IN_VMEM] * len(pieces),
        out_specs=pl.BlockSpec(memory_space=pltpu.HBM),
        scratch_shapes=[pltpu.SemaphoreType.DMA((len(pieces),))],
        compiler_params=pltpu.CompilerParams(vmem_limit_bytes=VMEM_LIMIT),
        name="put_together",
    )(place, *pieces)


def along_y(value, shift):
    size = lax.axis_size("grp")
    pairs = [(g, (g + 2 * shift) % size) for g in range(size)]
    return lax.ppermute(value, "grp", pairs)


def other_core(value):
    return lax.ppermute(value, "grp", [(g, g ^ 1) for g in range(lax.axis_size("grp"))])


def on_device(coefficients, source_blocks, target_blocks, pair_tables):
    group = lax.axis_index("grp")
    row, core = group >> 1, group & 1
    place = jnp.stack([row, core]).astype(jnp.int32)
    order = pair_tables.reshape(pair_tables.shape[0], pair_tables.shape[2])

    first_blocks = target_blocks[0]
    own_blocks = slice_blocks(place, target_blocks)
    moved = {shift: along_y(own_blocks[shift], shift) for shift in SHIFTS}
    blocks = [own_blocks[0], moved[1], moved[2], moved[3]]

    pieces = []
    for chunk, cols in enumerate(CHUNKS):
        state = source_levels(coefficients, source_blocks, order, sum(CHUNKS[:chunk]), cols)
        state = lax.all_to_all(state, "wide", split_axis=0, concat_axis=0, tiled=True)
        other = other_core(state)
        outs = core_level(place, state, other, first_blocks)
        arrived = {shift: along_y(outs[shift], shift) for shift in SHIFTS}
        states = [outs[0], arrived[1], arrived[2], arrived[3]]
        results = plane_levels(place, states, blocks)
        home = {shift: along_y(results[shift], shift) for shift in SHIFTS}
        pieces += [results[0], home[1], home[2], home[3]]
    return put_together(place, pieces, CHUNKS)


def solution(mesh):
    in_specs = (
        P(("grp", "wide"), None, None, None),
        P(None, ("grp", "wide"), None, None, None),
        P(None, ("grp", "wide"), None, None, None),
        P(None, ("grp", "wide"), None),
    )
    out_specs = P(("grp", "wide"), None, None, None)

    return jax.shard_map(
        on_device, mesh=mesh, in_specs=in_specs, out_specs=out_specs, check_vma=False
    )
```
